32 devices in a mesh: dp: 8 (over z, x), tensor: 4 (over y, core).
Axes of the slice: x: 2, y: 2, z: 4, core: 2. Of those that a mesh axis runs over, the one named last changes fastest.
Arguments:
- tokens: bfloat16 [8192, 2048], P('dp'), may hold values from -6 to 6
- segments: int32 [8, 1024], P('dp'), may hold values from 0 to 7, never falling along the last dimension, each value on 1 to 512 neighbouring positions
- keep: int32 [8, 2], P('dp'), may hold values 0 or 1
- rates: float32 [2], replicated, may hold values from 0.5 to 1
- gain_attn: float32 [2048], replicated, may hold values from 0.5 to 1.5
- w_query: bfloat16 [2048, 2048], P(None, 'tensor'), may hold values from -0.125 to 0.125
- w_key: bfloat16 [2048, 1024], P(None, 'tensor'), may hold values from -0.125 to 0.125
- w_value: bfloat16 [2048, 1024], P(None, 'tensor'), may hold values from -0.125 to 0.125
- w_out: bfloat16 [2048, 2048], P('tensor'), may hold values from -1 to 1
- gain_ffn: float32 [2048], replicated, may hold values from 0.5 to 1.5
- w_gate: bfloat16 [2048, 5632], P(None, 'tensor'), may hold values from -0.125 to 0.125
- w_up: bfloat16 [2048, 5632], P(None, 'tensor'), may hold values from -0.125 to 0.125
- w_down: bfloat16 [5632, 2048], P('tensor'), may hold values from -0.078125 to 0.078125
- cotangent: bfloat16 [8192, 2048], P('dp'), may hold values from -6 to 6
Outputs:
- layer_out: float32 [8192, 2048], P(('dp', 'tensor'))
- tokens_grad: float32 [8192, 2048], P(('dp', 'tensor'))
- gain_attn_grad: float32 [2048], P(('dp', 'tensor'))
- w_query_grad: float32 [2048, 2048], P('dp', 'tensor')
- w_key_grad: float32 [2048, 1024], P('dp', 'tensor')
- w_value_grad: float32 [2048, 1024], P('dp', 'tensor')
- w_out_grad: float32 [2048, 2048], P('tensor', 'dp')
- gain_ffn_grad: float32 [2048], P(('dp', 'tensor'))
- w_gate_grad: float32 [2048, 5632], P('dp', 'tensor')
- w_up_grad: float32 [2048, 5632], P('dp', 'tensor')
- w_down_grad: float32 [5632, 2048], P('tensor', 'dp')
The draws below stay inside these ranges and needn't reach their ends.
Inputs may be any that keep to these rules, and one draw needn't show every extreme that they name: `segments`: segment numbers never fall along a sequence; each of the 8 numbers covers 1 to 512 tokens, one exactly 512.
All inputs are finite; a program needn't handle non-finite values. No bound on the sum of `keep` on one device may be relied on, other than what follows from the above.
Results may differ from the reference program's by a relative error of at most 0.012.
Values may be sent and summed in bfloat16 or wider, within the bound.
No kernel may reach another device: no remote copies, remote signals or barrier semaphores. Data moves between devices by JAX's collectives and lax.ppermute only.
A program may use at most 256 MiB of HBM per device.

```python
import math
import jax
import jax.numpy as jnp
import numpy as np
from jax import lax

D = 2048
HQ = 16
KV = 8
HD = 128
FF = 5632
SEQ = 1024
DOCS = 8
MOST = 512
SEQS = 8
TOKENS = 8192


def plant(result, stream_key, least, high):
    shape = result.shape
    place = [jax.random.randint(jax.random.fold_in(stream_key, axis), (), 0, shape[axis]) for axis in range(len(shape))]
    result = result.at[tuple(place)].set(least)
    longest = shape.index(max(shape))
    place[longest] = (place[longest] + 1) % shape[longest]
    return result.at[tuple(place)].set(high)


def raised(values, own_key, source, target, parts, factor):
    owner, partner = [(jnp.arange(values.shape[dim]) // (values.shape[dim] // parts)).reshape([-1 if axis == dim else 1 for axis in range(values.ndim)]) for dim in (source, target)]
    chosen = jax.random.permutation(own_key, parts)[partner]
    strong = (owner == chosen) | (owner == (partner + parts // 2) % parts)
    return jnp.where(strong, factor * values, values)


def level_of(rng, shape, split, low, top_value):
    gain, own = 1.0, jax.random.fold_in(rng, 6)
    for dim, shards_of in split:
        draws = jnp.exp(jax.random.uniform(jax.random.fold_in(own, dim), (shards_of,), jnp.float32, low / len(split), top_value / len(split)))
        gain = gain * jnp.repeat(draws, shape[dim] // shards_of).reshape([-1 if axis == dim else 1 for axis in range(len(shape))])
    return gain


def profile(amount, total, limit, skew):
    weights = [(1 << 20) // math.isqrt(rank ** skew) + 1 for rank in range(2, amount + 1)]
    surplus, given = total - limit - (amount - 1), [1] * (amount - 1)
    while surplus > 0:
        candidates = [i for i in range(amount - 1) if given[i] < limit]
        whole, remaining = sum([weights[i] for i in candidates]), surplus
        for i in candidates:
            extra = min(limit - given[i], max(1, remaining * weights[i] // whole), surplus)
            given[i] = given[i] + extra
            surplus = surplus - extra
    return np.array([limit] + given)


def uneven(stream_key, amount, total, most, slope):
    if amount == 2:
        one = jax.random.randint(stream_key, (), max(1, total - most), min(most, total - 1) + 1)
        return jnp.stack([one, total - one])
    lengths = jnp.asarray(profile(amount, total, most, slope), jnp.int32)
    couples = (amount - 1) // 2
    giver, sink = lengths[1:1 + 2 * couples:2], lengths[2:2 + 2 * couples:2]
    slack = jnp.minimum(giver - 1, most - sink)
    moved = jax.random.randint(jax.random.fold_in(stream_key, 1), (couples,), 0, 1 << 20) % (slack + 1)
    lengths = lengths.at[1:1 + 2 * couples:2].set(giver - moved).at[2:2 + 2 * couples:2].set(sink + moved)
    return lengths[jax.random.permutation(jax.random.fold_in(stream_key, 2), amount)]


def scatter_about(key, extent, scale, reach, shards=(), kind=jnp.bfloat16):
    level = level_of(key, extent, shards, -0.22, 0.18) if shards else 1.0
    drawn = jax.random.normal(key, extent, jnp.float32) * scale * level
    return jnp.minimum(jnp.maximum(drawn, -reach), reach).astype(kind)


def noise_with(key, dims, scale, reach, shards, heavy, kind=jnp.bfloat16):
    values = scale * jax.random.normal(key, dims, jnp.float32)
    if shards:
        values = values * level_of(key, dims, shards, -0.22, 0.18)
    return jnp.clip(raised(values, jax.random.fold_in(key, 3), *heavy), -reach, reach).astype(kind)


def setup_inputs(seed: int = 0) -> dict:
    key_list = jax.random.split(jax.random.key(seed), 15)
    return {
        "tokens": noise_with(key_list[0], (TOKENS, D), 1.0, 6.0, ((0, 8),), (0, 1, 8, 2.0)),
        "segments": jax.vmap(lambda own: jnp.searchsorted(jnp.cumsum(uneven(own, DOCS, SEQ, MOST, 1)), jnp.arange(SEQ), side="right"))(jax.random.split(key_list[1], SEQS)).reshape((SEQS, SEQ)).astype(jnp.int32),
        "keep": plant((jax.random.randint(key_list[2], (SEQS, 2), 0, 4) < 3).astype(jnp.int32), jax.random.fold_in(key_list[2], 1), 0, 1),
        "rates": jnp.clip(jax.random.uniform(key_list[3], (2,), jnp.float32, 0.5, 1.0), 0.5, 1.0),
        "gain_attn": jnp.clip(1.0 + 0.1 * jax.random.normal(key_list[4], (D,), jnp.float32), 0.5, 1.5),
        "w_query": scatter_about(key_list[5], (D, HQ * HD), D ** -0.5, 0.125, ((1, 4),)),
        "w_key": scatter_about(key_list[6], (D, KV * HD), D ** -0.5, 0.125, ((1, 4),)),
        "w_value": scatter_about(key_list[7], (D, KV * HD), D ** -0.5, 0.125, ((1, 4),)),
        "w_out": scatter_about(key_list[8], (HQ * HD, D), (HQ * HD // 64) ** -0.5, 1.0, ((0, 4),)),
        "gain_ffn": jnp.clip(1.0 + 0.1 * jax.random.normal(key_list[9], (D,), jnp.float32), 0.5, 1.5),
        "w_gate": scatter_about(key_list[10], (D, FF), D ** -0.5, 0.125, ((1, 4),)),
        "w_up": scatter_about(key_list[11], (D, FF), D ** -0.5, 0.125, ((1, 4),)),
        "w_down": scatter_about(key_list[12], (FF, D), FF ** -0.5, 0.078125, ((0, 4),)),
        "cotangent": noise_with(key_list[13], (TOKENS, D), 1.0, 6.0, ((0, 8),), (0, 1, 8, 2.0)),
    }


@jax.custom_vjp
def low(v):
    return lax.optimization_barrier(v.astype(jnp.bfloat16)).astype(jnp.float32)

@jax.custom_vjp
def low_back(v):
    return v

def low_keep(v):
    return (low(v), None)

def low_pass(kept, grad):
    return (grad,)

def back_keep(v):
    return (v, None)

def back_low(kept, grad):
    return (low(grad),)
low.defvjp(low_keep, low_pass)
low_back.defvjp(back_keep, back_low)
epsilon = 1e-05
rope_base = 10000.0

def rotate_half(values):
    half = values.shape[-1] // 2
    return jnp.concatenate([-values[..., half:], values[..., :half]], axis=-1)

def rope_tables(segs):
    index = jnp.arange(segs.shape[0], dtype=jnp.int32)
    before = jnp.concatenate([segs[:1] - 1, segs[:-1]])
    starts = lax.cummax(jnp.where(segs != before, index, 0), axis=0)
    position = (index - starts).astype(jnp.float32)
    freqs = rope_base ** (-jnp.arange(HD // 2, dtype=jnp.float32) * 2.0 / HD)
    angles = position[:, None] * freqs[None, :]
    angles = jnp.concatenate([angles, angles], axis=-1)
    return (jnp.cos(angles)[:, None, :], jnp.sin(angles)[:, None, :])

def inv_rms(values):
    return lax.rsqrt(lax.optimization_barrier(jnp.mean(values * values, axis=-1, keepdims=True)) + epsilon)

def product(left, right):
    return jnp.dot(left, right, precision=lax.Precision.HIGHEST)

def one_sequence(inputs, segs, scales, params):
    gain_attn, w_query, w_key, w_value, w_out, gain_ffn, w_gate, w_up, w_down = params
    length = inputs.shape[0]
    angle_cos, angle_sin = rope_tables(segs)
    normed = low(inputs * inv_rms(inputs) * gain_attn)
    queries = low_back(product(normed, w_query)).reshape(length, HQ, HD)
    keys = low_back(product(normed, w_key)).reshape(length, KV, HD)
    values = low(low_back(product(normed, w_value))).reshape(length, KV, HD)
    queries = low(queries * angle_cos + rotate_half(queries) * angle_sin)
    keys = low(keys * angle_cos + rotate_half(keys) * angle_sin)
    queries = queries.reshape(length, KV, HQ // KV, HD)
    logits = jnp.einsum('sjgd,tjd->jgst', queries, keys, precision=lax.Precision.HIGHEST)
    logits = low_back(logits * HD ** (-0.5))
    index = jnp.arange(length, dtype=jnp.int32)
    allowed = (segs[:, None] == segs[None, :]) & (index[:, None] >= index[None, :])
    logits = jnp.where(allowed, logits, -1e+30)
    probs = low(jax.nn.softmax(logits, axis=-1))
    attended = jnp.einsum('jgst,tjd->sjgd', probs, values, precision=lax.Precision.HIGHEST)
    attended = low(low_back(attended.reshape(length, HQ * HD)))
    branch = low_back(product(attended, w_out))
    middle = inputs + scales[0] * branch
    normed_ffn = low(middle * inv_rms(middle) * gain_ffn)
    gate = low_back(product(normed_ffn, w_gate))
    upward = low_back(product(normed_ffn, w_up))
    hidden = low(jax.nn.silu(gate) * upward)
    ffn_out = low_back(product(hidden, w_down))
    return middle + scales[1] * ffn_out

def reference(tokens, segments, keep, rates, gain_attn, w_query, w_key, w_value, w_out, gain_ffn, w_gate, w_up, w_down, cotangent):
    inputs = tokens.astype(jnp.float32).reshape(SEQS, SEQ, D)
    params = tuple((p.astype(jnp.float32) for p in (gain_attn, w_query, w_key, w_value, w_out, gain_ffn, w_gate, w_up, w_down)))
    scales = keep.astype(jnp.float32) / rates[None, :].astype(jnp.float32)

    def forward(inputs, params):

        def step(carry, item):
            seq_in, seq_segs, seq_scales = item
            return (carry, jax.checkpoint(one_sequence)(seq_in, seq_segs, seq_scales, params))
        _, outputs = lax.scan(step, None, (inputs, segments, scales))
        return outputs
    outputs, pull = jax.vjp(forward, inputs, params)
    input_grad, grads = pull(cotangent.astype(jnp.float32).reshape(SEQS, SEQ, D))
    return (outputs.reshape(TOKENS, D), input_grad.reshape(TOKENS, D), grads[0], grads[1], grads[2], grads[3], grads[4], grads[5], grads[6], grads[7], grads[8])
```

```python
import functools

import jax
import jax.numpy as jnp
from jax import lax
from jax.experimental import pallas as pl
from jax.experimental.pallas import tpu as pltpu
from jax.sharding import PartitionSpec as P

HD = 128
CORE, CHIP = 0, 1

epsilon = 1e-05
rope_base = 10000.0


def rope_tables(start):
    length = start.shape[1]
    position = (jnp.arange(length, dtype=jnp.int32) - start[0]).astype(jnp.float32)
    freqs = rope_base ** (-jnp.arange(HD // 2, dtype=jnp.float32) * 2.0 / HD)
    angles = position[:, None] * freqs[None, :]
    cos, sin = jnp.cos(angles), jnp.sin(angles)
    return jnp.concatenate([cos, cos], axis=-1), jnp.concatenate([-sin, sin], axis=-1)


def inv_rms(values):
    return lax.rsqrt(jnp.mean(values * values, axis=-1, keepdims=True) + epsilon)


def product(left, right):
    return jnp.dot(left, right, preferred_element_type=jnp.float32)


def product_tn(left, right):
    return lax.dot_general(
        left, right, (((0,), (0,)), ((), ())), preferred_element_type=jnp.float32
    )


def product_nt(left, right):
    return lax.dot_general(
        left, right, (((1,), (1,)), ((), ())), preferred_element_type=jnp.float32
    )


def norm_back(grad, inputs, inverse, gain):
    weighted = grad * gain
    return inverse * weighted - inputs * inverse**3 * jnp.mean(
        weighted * inputs, axis=-1, keepdims=True
    )


def low(values):
    return values.astype(jnp.bfloat16)


def wide(values):
    return values.astype(jnp.float32)


def part(values, start, stop, dim):
    return lax.slice_in_dim(values, start, stop, axis=dim)


class Chain:
    def __init__(self):
        self.token = None
        self.count = 0
        self.moved = (0, 0)

    def __call__(self, step, *operands):
        if self.token is not None:
            operands, _ = lax.optimization_barrier((operands, self.token))
        self.count += 1
        result = step(*operands)
        self.token = result
        return result

    def move(self, values, axis, pairs):
        values, _ = lax.optimization_barrier((values, self.token))
        if self.moved[0] != self.count:
            self.moved = (self.count, 0)
        part = self.moved[1]
        self.moved = (self.count, part + 1)
        return lax.ppermute(values, axis, pairs)

    def flip(self, values, axis, bit):
        return self.move(values, axis, [(i, i ^ (1 << bit)) for i in range(lax.axis_size(axis))])


class Piece:
    def __init__(self, chain, left, right, width, dim):
        self.chain, self.left, self.right, self.width, self.dim = chain, left, right, width, dim
        self.mine = lax.axis_index("dp")
        self.total = None
        self.todo = list(self.stages)

    def go(self):
        if self.todo:
            stage, self.todo = self.todo[0], self.todo[1:]
            getattr(self, stage)()

    def result(self):
        while self.todo:
            self.go()
        return self.total

    columns_of = None

    def products(self, blocks, dtype, *terms, columns_of=None):
        arrays, places = [t for t, _ in terms], [p for _, p in terms]

        def step(left, right, *arrays):
            return grad(
                left,
                right,
                blocks,
                self.width,
                self.dim,
                dtype,
                list(zip(arrays, places)),
                columns_of,
            )

        return self.chain(step, self.left, self.right, *arrays)


class Halving(Piece):
    def __init__(self, chain, left, right, width, dim, orders, split=()):
        self.orders, self.size = orders, 1 << len(orders[0])
        depth = len(orders[0])
        self.masks = [
            [
                sum(1 << order[s] for s in range(depth) if p >> (depth - 1 - s) & 1)
                for p in range(self.size)
            ]
            for order in orders
        ]
        self.stages, self.sends = [], []
        for step in range(depth):
            half = self.size >> (step + 1)
            cuts = [0, half // 2, half] if step in split and half > 1 else [0, half]
            self.sends += [(step, half, a, b) for a, b in list(zip(cuts, cuts[1:]))[::-1]]
        self.stages = ["send"] * len(self.sends) + ["last"]
        self.received = []
        super().__init__(chain, left, right, width, dim)

    def positions(self, a, b, dtype, **options):
        terms = [(r, a - at) for at, to, r in self.received if at <= a and b <= to]
        core = lax.axis_index("tensor") & 1
        blocks = [
            self.mine ^ (m if m == other else jnp.where(core == 0, m, other))
            for m, other in zip(self.masks[0][a:b], self.masks[1][a:b])
        ]
        return self.products(blocks, dtype, *terms, **options)

    def send(self):
        step, half, a, b = self.sends.pop(0)
        top = self.positions(half + a, half + b, jnp.bfloat16)
        cores = lax.axis_size("tensor")
        pairs = [
            (i * cores + t, (i ^ (1 << self.orders[t & 1][step])) * cores + t)
            for i in range(lax.axis_size("dp"))
            for t in range(cores)
        ]
        self.received.append((a, b, self.chain.move(top, ("dp", "tensor"), pairs)))

    def last(self):
        self.total = self.positions(0, 1, jnp.float32, columns_of=self.columns_of)


def take(values, blocks, width):
    return jnp.concatenate(
        [lax.dynamic_slice_in_dim(values, block * width, width, 1) for block in blocks], axis=1
    )


LOG2E = 1.4426950408889634
SPAN = 512
TILE = 256
COLUMNS = 512
NEG = -1e30


def whole_block(array):
    zeros = (0,) * array.ndim
    return pl.BlockSpec(array.shape, lambda *_: zeros)


def project_kernel(x_ref, gain_ref, wq_ref, wk_ref, wv_ref, cos_ref, sin_ref, n_ref, q_ref, k_ref, v_ref):
    x = wide(x_ref[...])
    inverse = lax.rsqrt(jnp.mean(x * x, axis=-1, keepdims=True) + epsilon)
    normed = low(x * inverse * gain_ref[...])
    n_ref[...] = normed
    cos, sin = cos_ref[...], sin_ref[...]
    for w_ref, o_ref in ((wq_ref, q_ref), (wk_ref, k_ref)):
        linear = product(normed, w_ref[...])
        for h in range(w_ref.shape[1] // HD):
            head = linear[:, h * HD : (h + 1) * HD]
            o_ref[:, h * HD : (h + 1) * HD] = low(head * cos + pltpu.roll(head, HD // 2, 1) * sin)
    v_ref[...] = low(product(normed, wv_ref[...]))


def project(tokens, gain, w_query, w_key, w_value, cos, sin):
    length, model = tokens.shape
    outs = (model, w_query.shape[1], w_key.shape[1], w_value.shape[1])
    rows = lambda columns: pl.BlockSpec((TILE, columns), lambda i: (i, 0))
    gain = gain.reshape(1, model)
    total = sum(outs[1:])
    return pl.pallas_call(
        project_kernel,
        grid=(length // TILE,),
        in_specs=[
            rows(model),
            whole_block(gain),
            whole_block(w_query),
            whole_block(w_key),
            whole_block(w_value),
            rows(HD),
            rows(HD),
        ],
        out_specs=[rows(columns) for columns in outs],
        out_shape=[jax.ShapeDtypeStruct((length, columns), jnp.bfloat16) for columns in outs],
        cost_estimate=pl.CostEstimate(
            flops=2 * length * model * total,
            bytes_accessed=2 * (2 * length * model + model * total + length * total),
            transcendentals=length,
        ),
        name="project",
    )(tokens, gain, w_query, w_key, w_value, cos, sin)


def span(i):
    return max(0, i * TILE - SPAN), (i + 1) * TILE


def allowed_keys(i, start_ref):
    low_key, high_key = span(i)
    shape = (high_key - low_key, TILE)
    key = lax.broadcasted_iota(jnp.int32, shape, 0) + low_key
    query = lax.broadcasted_iota(jnp.int32, shape, 1) + i * TILE
    return (key >= start_ref[:, i * TILE : (i + 1) * TILE]) & (key <= query)


def attend_kernel(half_ref, q_ref, k_ref, v_ref, start_ref, *refs):
    o_ref, lse_ref = refs[-2:]
    scale = HD**-0.5 * LOG2E
    heads = q_ref.shape[1] // HD
    rows = q_ref.shape[0]
    halves = k_ref.shape[0] // rows

    def tile(i):
        low_key, high_key = span(i)
        here = slice(i * TILE % rows, i * TILE % rows + TILE)
        allowed = allowed_keys(i, start_ref)
        values = low(jnp.transpose(wide(v_ref[low_key:high_key, :])))
        for h in range(heads):
            columns = slice(h * HD, (h + 1) * HD)
            logits = product_nt(k_ref[low_key:high_key, :], q_ref[here, columns]) * scale
            logits = jnp.where(allowed, logits, NEG)
            highest = jnp.max(logits, axis=0, keepdims=True)
            weights = jnp.exp2(logits - highest)
            total = jnp.sum(weights, axis=0, keepdims=True)
            probs = low(weights * (1.0 / total))
            o_ref[here, columns] = low(jnp.transpose(product(values, probs)))
            lse_ref[0, h : h + 1, here] = highest + jnp.log2(total)

    for half in range(halves):

        @pl.when(half_ref[0] == half)
        def _():
            for i in range(half * rows // TILE, (half + 1) * rows // TILE):
                tile(i)


def attend(queries, keys, values, start, half, earlier=()):
    length = queries.shape[0]
    rows = length // 2
    kv = keys.shape[1] // HD
    group = queries.shape[1] // keys.shape[1]
    return pl.pallas_call(
        attend_kernel,
        grid_spec=pltpu.PrefetchScalarGridSpec(
            num_scalar_prefetch=1,
            grid=(kv,),
            in_specs=[
                pl.BlockSpec((rows, group * HD), lambda j, half: (half[0], j)),
                pl.BlockSpec((length, HD), lambda j, half: (0, j)),
                pl.BlockSpec((length, HD), lambda j, half: (0, j)),
                whole_block(start),
            ]
            + [pl.BlockSpec(memory_space=pl.ANY)] * len(earlier),
            out_specs=[
                pl.BlockSpec((rows, group * HD), lambda j, half: (half[0], j)),
                pl.BlockSpec((1, group, rows), lambda j, half: (j, 0, half[0])),
            ],
        ),
        out_shape=[
            jax.ShapeDtypeStruct(queries.shape, jnp.bfloat16),
            jax.ShapeDtypeStruct((kv, group, length), jnp.float32),
        ],
        input_output_aliases={5 + i: i for i in range(len(earlier))},
        cost_estimate=pl.CostEstimate(
            flops=2 * length * SPAN * queries.shape[1],
            bytes_accessed=2 * (queries.size + 2 * keys.size),
            transcendentals=length * SPAN * kv * group // 2,
        ),
        name="attend",
    )(half.reshape(1), queries, keys, values, start, *earlier)


def attend_back_kernel(
    kv, q_ref, k_ref, v_ref, start_ref, lse_ref, g_ref, cos_ref, sin_ref, d_ref, k_sum, v_sum
):
    scale = HD**-0.5
    heads = q_ref.shape[1] // HD
    k_sum[...] = jnp.zeros_like(k_sum)
    v_sum[...] = jnp.zeros_like(v_sum)
    k_t = jnp.transpose(wide(k_ref[...]))
    j = pl.program_id(0)

    def columns_at(place):
        return pl.ds(pl.multiple_of(place * HD, HD), HD)

    def unrope(values, here):
        return low(
            values * cos_ref[here, :] - pltpu.roll(values, HD // 2, 1) * sin_ref[here, :]
        )

    for i in range(q_ref.shape[0] // TILE):
        low_key, high_key = span(i)
        here = slice(i * TILE, (i + 1) * TILE)
        reach = slice(low_key, high_key)
        allowed = allowed_keys(i, start_ref)
        for h in range(heads):
            columns = slice(h * HD, (h + 1) * HD)
            query, grad = q_ref[here, columns], g_ref[here, columns]
            logits = product_nt(k_ref[reach, :], query) * (scale * LOG2E)
            logits = jnp.where(allowed, logits - lse_ref[0, h : h + 1, here], NEG)
            probs = jnp.exp2(logits)
            d_probs = product_nt(v_ref[reach, :], grad)
            row_sum = jnp.sum(d_probs * probs, axis=0, keepdims=True)
            d_logits = low(probs * (d_probs - row_sum))
            v_sum[reach, :] += product(low(probs), grad)
            k_sum[reach, :] += product(d_logits, query)
            d_query = jnp.transpose(product(low(k_t[:, reach]), d_logits)) * scale
            d_ref[here, columns_at(j * heads + h)] = unrope(d_query, here)
    everything = slice(0, k_sum.shape[0])
    d_ref[:, columns_at(kv * heads + j)] = unrope(k_sum[...] * scale, everything)
    d_ref[:, columns_at(kv * (heads + 1) + j)] = low(v_sum[...])


def attend_back(queries, keys, values, start, log_total, grads, cos, sin):
    length = queries.shape[0]
    kv = keys.shape[1] // HD
    group = queries.shape[1] // keys.shape[1]
    total = queries.shape[1] + 2 * keys.shape[1]
    wide_block = pl.BlockSpec((length, group * HD), lambda j: (0, j))
    one_block = pl.BlockSpec((length, HD), lambda j: (0, j))
    return pl.pallas_call(
        functools.partial(attend_back_kernel, kv),
        grid=(kv,),
        in_specs=[
            wide_block,
            one_block,
            one_block,
            whole_block(start),
            pl.BlockSpec((1, group, length), lambda j: (j, 0, 0)),
            wide_block,
            whole_block(cos),
            whole_block(sin),
        ],
        out_specs=pl.BlockSpec((length, total), lambda j: (0, 0)),
        out_shape=jax.ShapeDtypeStruct((length, total), jnp.bfloat16),
        scratch_shapes=[pltpu.VMEM((length, HD), jnp.float32)] * 2,
        cost_estimate=pl.CostEstimate(
            flops=5 * length * SPAN * queries.shape[1] * 2,
            bytes_accessed=2 * (3 * queries.size + 4 * keys.size),
            transcendentals=length * SPAN * kv * group,
        ),
        name="attend_back",
    )(queries, keys, values, start, log_total, grads, cos, sin)


def grad_kernel(by_right, outs, blocks_ref, left_ref, right_ref, *refs):
    refs = list(refs)
    turned = refs.pop() if by_right else None
    out_refs, refs = refs[-outs:], refs[:-outs]
    if by_right:

        @pl.when(pl.program_id(0) == 0)
        def _():
            turned[...] = low(jnp.transpose(wide(left_ref[...])))

        total = product(turned[...], right_ref[...])
    else:
        total = product_tn(left_ref[...], right_ref[...])
    for ref in refs:
        total = total + wide(ref[...])
    place = 0
    for out_ref in out_refs:
        columns = out_ref.shape[1]
        out_ref[...] = total[:, place : place + columns].astype(out_ref.dtype)
        place += columns


def grad(left, right, blocks, width, dim, dtype, terms=(), columns_of=None):
    count = len(blocks)
    tokens = left.shape[0]
    rows, columns = left.shape[1], right.shape[1]
    if width % HD:
        if dim == 0:
            left = take(left, blocks, width)
        else:
            right = take(right, blocks, width)
        total = product_tn(left, right)
        for term, place in terms:
            total = total + wide(part(term, place * width, (place + count) * width, dim))
        total = total.astype(dtype)
        if columns_of is None:
            return total
        return jnp.split(total, [sum(columns_of[: i + 1]) for i in range(len(columns_of) - 1)], axis=1)
    by_right = dim == 1
    pick = lambda p, blocks: (0, blocks[p])
    fixed = lambda p, blocks: (0, 0)
    if by_right:
        left_spec, right_spec = pl.BlockSpec((tokens, rows), fixed), pl.BlockSpec((tokens, width), pick)
        shape, block = (rows, count * width), (rows, width)
        at = lambda place: lambda p, blocks: (0, place + p)
    else:
        left_spec, right_spec = pl.BlockSpec((tokens, width), pick), pl.BlockSpec((tokens, columns), fixed)
        shape, block = (count * width, columns), (width, columns)
        at = lambda place: lambda p, blocks: (place + p, 0)
    return pl.pallas_call(
        functools.partial(grad_kernel, by_right, len(columns_of) if columns_of else 1),
        grid_spec=pltpu.PrefetchScalarGridSpec(
            num_scalar_prefetch=1,
            grid=(count,),
            in_specs=[left_spec, right_spec] + [pl.BlockSpec(block, at(place)) for _, place in terms],
            out_specs=[pl.BlockSpec((block[0], c), at(0)) for c in columns_of]
            if columns_of
            else pl.BlockSpec(block, at(0)),
            scratch_shapes=[pltpu.VMEM((rows, tokens), jnp.bfloat16)] if by_right else [],
        ),
        out_shape=[jax.ShapeDtypeStruct((shape[0], c), dtype) for c in columns_of]
        if columns_of
        else jax.ShapeDtypeStruct(shape, dtype),
        cost_estimate=pl.CostEstimate(
            flops=2 * tokens * shape[0] * shape[1],
            bytes_accessed=2 * (tokens * (shape[0] + shape[1]) + (1 + len(terms)) * shape[0] * shape[1]),
            transcendentals=0,
        ),
        name="grad",
    )(jnp.stack(blocks), left, right, *(term for term, _ in terms))


def middle_kernel(place_ref, scale_ref, gain_ref, x_ref, own_ref, near_ref, far_ref, *refs):
    m_ref, inv_ref, n_ref = refs[-3:]
    branch = wide(own_ref[...]) + wide(near_ref[...]) + wide(far_ref[...])
    middle = wide(x_ref[...]) + scale_ref[0] * branch
    inverse = lax.rsqrt(jnp.mean(middle * middle, axis=-1, keepdims=True) + epsilon)
    m_ref[...] = middle
    inv_ref[...] = inverse
    n_ref[...] = low(middle * inverse * gain_ref[...])


def middle_of(chunk, tokens, own, near, far, mine, scale, gain, earlier=()):
    share, model = own.shape
    tile = far.shape[0]
    gain = gain.reshape(1, model)
    at = lambda i, place: (chunk, 0)
    only = lambda i, place: (0, 0)
    return pl.pallas_call(
        middle_kernel,
        grid_spec=pltpu.PrefetchScalarGridSpec(
            num_scalar_prefetch=1,
            grid=(1,),
            in_specs=[
                pl.BlockSpec(memory_space=pltpu.SMEM),
                whole_block(gain),
                pl.BlockSpec((tile, model), lambda i, place: (place[0] * (share // tile) + chunk, 0)),
                pl.BlockSpec((tile, model), at),
                pl.BlockSpec((tile, model), at),
                pl.BlockSpec((tile, model), only),
            ]
            + [pl.BlockSpec(memory_space=pl.ANY)] * len(earlier),
            out_specs=[
                pl.BlockSpec((tile, model), at),
                pl.BlockSpec((tile, 1), at),
                pl.BlockSpec((tile, model), only),
            ],
        ),
        out_shape=[
            jax.ShapeDtypeStruct((share, model), jnp.float32),
            jax.ShapeDtypeStruct((share, 1), jnp.float32),
            jax.ShapeDtypeStruct((tile, model), jnp.bfloat16),
        ],
        input_output_aliases={7 + i: i for i in range(len(earlier))},
        cost_estimate=pl.CostEstimate(
            flops=10 * tile * model, bytes_accessed=14 * tile * model, transcendentals=tile
        ),
        name="middle",
    )(mine.reshape(1), scale.reshape(1), gain, tokens, own, near, far, *earlier)


def gated_kernel(count, places_ref, *refs):
    pieces, (dh_ref, wg_ref, wu_ref) = refs[: 2 * count], refs[2 * count : 2 * count + 3]
    n_ref, hidden_ref, dg_ref, du_ref = refs[-4:]
    core = places_ref[1]

    @pl.when(pl.program_id(0) == 0)
    def _():
        tile = pieces[0].shape[0]
        for i in range(count):
            for place, piece in ((core, pieces[i]), (1 - core, pieces[count + i])):
                row = pl.multiple_of((place * count + i) * tile, tile)
                n_ref[pl.ds(row, tile), :] = piece[...]

    gate = product(n_ref[...], wg_ref[...])
    upward = product(n_ref[...], wu_ref[...])
    d_hidden = dh_ref[...]
    sigma = jax.nn.sigmoid(gate)
    silu = gate * sigma
    hidden_ref[...] = low(silu * upward)
    du_ref[...] = low(d_hidden * silu)
    dg_ref[...] = low(d_hidden * upward * sigma * (1.0 + gate * (1.0 - sigma)))


def gated(chip, core, own, near, d_hidden, w_gate, w_up, earlier=()):
    count = len(own)
    rows = 2 * count * own[0].shape[0]
    length, hidden = d_hidden.shape
    model = w_gate.shape[0]
    whole = lambda array: pl.BlockSpec(array.shape, lambda n, places: (0, 0))
    block = pl.BlockSpec((rows, COLUMNS), lambda n, places: (places[0], n))
    weight = pl.BlockSpec((model, COLUMNS), lambda n, places: (0, n))
    pieces = [*own, *near]
    return pl.pallas_call(
        functools.partial(gated_kernel, count),
        grid_spec=pltpu.PrefetchScalarGridSpec(
            num_scalar_prefetch=1,
            grid=(pl.cdiv(hidden, COLUMNS),),
            in_specs=[whole(piece) for piece in pieces]
            + [block, weight, weight]
            + [pl.BlockSpec(memory_space=pl.ANY)] * len(earlier),
            out_specs=[pl.BlockSpec((rows, model), lambda n, places: (places[0], 0))]
            + [block] * 3,
        ),
        out_shape=[jax.ShapeDtypeStruct((length, model), jnp.bfloat16)]
        + [jax.ShapeDtypeStruct((length, hidden), jnp.bfloat16)] * 3,
        input_output_aliases={4 + 2 * count + i: i for i in range(len(earlier))},
        cost_estimate=pl.CostEstimate(
            flops=4 * rows * model * hidden,
            bytes_accessed=2 * (2 * rows * model + 2 * model * hidden + 5 * rows * hidden),
            transcendentals=rows * hidden,
        ),
        name="gated",
    )(jnp.stack([chip, core]), *pieces, d_hidden, w_gate, w_up, *earlier)


def branch_back_kernel(places_ref, *refs):
    w_ref, d_ref, a_ref = refs[-3:]
    for i, ref in enumerate(refs[:-3]):

        @pl.when(pl.program_id(0) == i)
        def _():
            d_ref[...] = ref[...]

    a_ref[...] = low(product_nt(d_ref[...], w_ref[...]))


def branch_back(pieces, places, w_out):
    rows, model = pieces[0].shape
    count = len(pieces)
    heads = w_out.shape[0]
    fixed = lambda array: pl.BlockSpec(array.shape, lambda p, places: (0, 0))
    return pl.pallas_call(
        branch_back_kernel,
        grid_spec=pltpu.PrefetchScalarGridSpec(
            num_scalar_prefetch=1,
            grid=(count,),
            in_specs=[fixed(piece) for piece in pieces] + [fixed(w_out)],
            out_specs=[
                pl.BlockSpec((rows, model), lambda p, places: (places[p], 0)),
                pl.BlockSpec((rows, heads), lambda p, places: (places[p], 0)),
            ],
        ),
        out_shape=[
            jax.ShapeDtypeStruct((count * rows, model), jnp.bfloat16),
            jax.ShapeDtypeStruct((count * rows, heads), jnp.bfloat16),
        ],
        cost_estimate=pl.CostEstimate(
            flops=2 * count * rows * model * heads,
            bytes_accessed=2 * (2 * count * rows * model + heads * model),
            transcendentals=0,
        ),
        name="branch_back",
    )(jnp.stack(places), *pieces, w_out)


class Scatter:
    def __init__(self, chain, make, left, *operands):
        self.chain, self.make, self.left, self.operands = chain, make, left, operands
        self.share = left[0].shape[0] // 4
        self.mine = lax.axis_index("tensor")
        self.chip, self.core = self.mine >> 1, self.mine & 1

    def rows(self, place, count):
        def step(left, *operands):
            left = [
                lax.dynamic_slice_in_dim(v, place * self.share, count * self.share, 0) for v in left
            ]
            return low(self.make(left, *operands))

        return self.chain(step, self.left, *self.operands)

    def far_half(self):
        self.half = self.rows((1 - self.chip) * 2, 2)
        self.half_near = self.chain.flip(self.half, "tensor", CORE)

    def near_half(self):
        self.own = self.rows(self.chip * 2, 2)
        self.near = self.chain.flip(self.own, "tensor", CORE)

    def far_rows(self):
        self.half_near = self.chain.flip(self.rows(self.mine ^ 3, 1), "tensor", CORE)
        self.half = self.rows(self.mine ^ 2, 1)

    def near_rows(self):
        self.near = self.chain.flip(self.rows(self.mine ^ 1, 1), "tensor", CORE)
        self.own = self.rows(self.mine, 1)

    def mine_of(self, values):
        if values.shape[0] == self.share:
            return values
        return lax.dynamic_slice_in_dim(values, self.core * self.share, self.share, 0)

    def far_send(self):
        total = self.chain(
            lambda a, b: low(wide(self.mine_of(a)) + wide(self.mine_of(b))), self.half, self.half_near
        )
        self.from_far = self.chain.flip(total, "tensor", CHIP)

    def parts(self):
        return self.own, self.near, self.from_far

    def total(self, parts):
        own, near, far = parts
        return wide(self.mine_of(own)) + wide(self.mine_of(near)) + wide(far)


def keep_half(values, axis, dim, bit):
    shape = values.shape
    split = values.reshape(*shape[:dim], shape[dim] // 2, 2, *shape[dim + 1 :])
    mine = (lax.axis_index(axis) >> bit) & 1
    return (
        lax.dynamic_index_in_dim(split, mine, dim + 1, keepdims=False),
        lax.dynamic_index_in_dim(split, 1 - mine, dim + 1, keepdims=False),
    )


class SmallScatter:
    def __init__(self, chain, values, dp, ts):
        self.chain, self.values = chain, values
        self.bits = [("tensor", 2, b) for b in range(ts.bit_length() - 1)]
        self.bits += [("dp", 1, b) for b in range(dp.bit_length() - 1)]
        self.arrived = None

    def step(self):
        if not self.bits:
            return
        (axis, dim, bit), self.bits = self.bits[0], self.bits[1:]

        def halve(values, arrived):
            if arrived is not None:
                values = values + arrived
            return keep_half(values, axis, dim, bit)

        self.values, send = self.chain(halve, self.values, self.arrived)
        self.arrived = self.chain.flip(send, axis, bit)

    def last(self):
        while self.bits:
            self.step()
        return self.chain(lambda a, b: a + b, self.values, self.arrived)[:, 0, 0]


def shards(*arrays):
    return block(Chain(), *arrays)


def block(
    chain,
    tokens,
    segments,
    keep,
    rates,
    gain_attn,
    w_query,
    w_key,
    w_value,
    w_out,
    gain_ffn,
    w_gate,
    w_up,
    w_down,
    cotangent,
):
    length, model = tokens.shape
    dp = lax.axis_size("dp")
    ts = lax.axis_size("tensor")
    share = length // ts
    mine = lax.axis_index("tensor")
    chip, core = mine >> 1, mine & 1
    first = mine * share
    width = model // dp
    segs = segments[0]
    start = jnp.sum((segs[:, None] < segs[None, :]).astype(jnp.int32), axis=0, keepdims=True)
    cos, sin = rope_tables(start)

    normed, queries, keys, values = chain(
        project, tokens, gain_attn, w_query, w_key, w_value, cos, sin
    )
    earlier = chain(attend, queries, keys, values, start, 1 - chip)
    branch = Scatter(chain, lambda left, w: product(left[0], w), [earlier[0]], w_out)
    branch.far_rows()
    tile = share // 2
    chunks = [(c * tile, (c + 1) * tile, 0) for c in range(2)]
    totals = chain(
        lambda a, b: [low(wide(part(a, *c)) + wide(part(b, *c))) for c in chunks],
        branch.half,
        branch.half_near,
    )
    arrived = [chain.flip(total, "tensor", CHIP) for total in totals]
    attended, log_total = chain(
        lambda *o: attend(*o[:5], o[5]), queries, keys, values, start, chip, tuple(earlier)
    )
    branch.left = [attended]
    branch.near_rows()

    def prepare(keep, rates, cotangent):
        scales = keep[0].astype(jnp.float32) / rates
        return scales[0], scales[1], low(scales[1] * wide(cotangent))

    scale_attn, scale_ffn, d_ffn = chain(prepare, keep, rates, cotangent)
    far, near, own, outs = [], [], [], ()
    for c in range(2):
        *outs, normed_rows = chain(
            lambda *o: middle_of(c, *o),
            tokens,
            branch.own,
            branch.near,
            arrived[c],
            mine,
            scale_attn,
            gain_ffn,
            tuple(outs),
        )
        own.append(normed_rows)
        far.append(chain.flip(normed_rows, "tensor", CHIP))
        near.append(chain.flip(normed_rows, "tensor", CORE))
        if c == 0:
            d_hidden = chain(product_nt, d_ffn, w_down)
    middle_rows, inv_mid_rows = outs
    outs = chain(gated, chip, core, own, near, d_hidden, w_gate, w_up)
    far_near = [chain.flip(f, "tensor", CORE) for f in far]
    normed_ffn, hidden, d_gate, d_up = chain(
        gated, 1 - chip, core, far, far_near, d_hidden, w_gate, w_up, tuple(outs)
    )
    bits = list(range(dp.bit_length() - 1))
    swapped = bits[:1] + bits[1:3][::-1] + bits[3:]

    def over_dp(left, right, dim, split=(), order=lambda v: v):
        return Halving(chain, left, right, width, dim, (order(bits), order(swapped)), split)

    gate_g = over_dp(normed_ffn, d_gate, 0)
    up_g = over_dp(normed_ffn, d_up, 0)
    down_g = over_dp(hidden, d_ffn, 1, split=(1,), order=lambda v: [v[1], v[0]] + v[2:])
    gate_g.go()
    down_g.go()

    d_normed = Scatter(
        chain,
        lambda left, g, u: product_nt(left[0], g) + product_nt(left[1], u),
        [d_gate, d_up],
        w_gate,
        w_up,
    )
    ffn = Scatter(chain, lambda left, w: product(left[0], w), [hidden], w_down)
    d_normed.far_half()
    up_g.go()
    d_normed.far_send()
    d_normed.near_half()
    ffn.far_half()

    def middle_back(parts, middle_rows, inv_mid_rows, cotangent):
        d_normed_rows = d_normed.total(parts)
        grad_rows = wide(lax.dynamic_slice_in_dim(cotangent, first, share, 0))
        d_middle_rows = grad_rows + norm_back(d_normed_rows, middle_rows, inv_mid_rows, gain_ffn)
        gain_ffn_part = jnp.sum(d_normed_rows * middle_rows * inv_mid_rows, axis=0)
        return d_middle_rows, low(scale_attn * d_middle_rows), gain_ffn_part

    d_middle_rows, d_branch_rows, gain_ffn_part = chain(
        middle_back, d_normed.parts(), middle_rows, inv_mid_rows, cotangent
    )
    far = chain.flip(d_branch_rows, "tensor", CHIP)
    near = chain.flip(d_branch_rows, "tensor", CORE)
    ffn.far_send()
    gate_g.go()
    down_g.go()
    ffn.near_half()
    far_near = chain.flip(far, "tensor", CORE)
    d_branch, d_attended = chain(
        lambda *o: branch_back(o[:4], [mine, mine ^ 1, mine ^ 2, mine ^ 3], o[4]),
        d_branch_rows,
        near,
        far,
        far_near,
        w_out,
    )
    wout_g = over_dp(attended, d_branch, 1)
    wout_g.go()
    gate_g.go()
    d_qkv = chain(attend_back, queries, keys, values, start, log_total, d_attended, cos, sin)
    qkv_g = over_dp(normed, d_qkv, 0, split=(0, 1))
    qkv_g.columns_of = (w_query.shape[1], w_key.shape[1], w_value.shape[1])
    qkv_g.go()
    up_g.go()
    qkv_g.go()
    down_g.go()
    q_cols, k_cols = w_query.shape[1], w_key.shape[1]

    def d_first_of(left, w_query, w_key, w_value):
        d_rows = left[0]
        return (
            product_nt(d_rows[:, :q_cols], w_query)
            + product_nt(d_rows[:, q_cols : q_cols + k_cols], w_key)
            + product_nt(d_rows[:, q_cols + k_cols :], w_value)
        )

    d_first = Scatter(chain, d_first_of, [d_qkv], w_query, w_key, w_value)
    d_first.far_rows()
    d_first.far_send()
    d_first.near_rows()
    down_g.go()
    wout_g.go()
    grad_gate = gate_g.result() if len(bits) == 3 else None

    def input_back(parts, tokens, d_middle_rows):
        d_first_rows = d_first.total(parts)
        input_rows = wide(lax.dynamic_slice_in_dim(tokens, first, share, 0))
        inv_in_rows = inv_rms(input_rows)
        tokens_grad = d_middle_rows + norm_back(d_first_rows, input_rows, inv_in_rows, gain_attn)
        return tokens_grad, jnp.sum(d_first_rows * input_rows * inv_in_rows, axis=0)

    tokens_grad, gain_attn_part = chain(input_back, d_first.parts(), tokens, d_middle_rows)
    gains = SmallScatter(
        chain, jnp.stack([gain_attn_part, gain_ffn_part]).reshape(2, dp, ts, -1), dp, ts
    )
    gains.step()
    gains.step()
    qkv_g.go()
    qkv_g.go()
    up_g.go()
    gains.step()
    wout_g.go()
    layer_out = chain(lambda m, f: m + scale_ffn * ffn.total(f), middle_rows, ffn.parts())
    gains.step()
    qkv_g.go()
    grad_down = down_g.result()
    for _ in range(len(bits) - 3):
        for piece in (gate_g, up_g, wout_g, qkv_g):
            piece.go()
    if grad_gate is None:
        grad_gate = gate_g.result()
    grad_up = up_g.result()
    grad_wout = wout_g.result()
    gains.step()
    grad_query, grad_key, grad_value = qkv_g.result()
    gains = gains.last()
    return (
        layer_out,
        tokens_grad,
        gains[0],
        grad_query,
        grad_key,
        grad_value,
        grad_wout,
        gains[1],
        grad_gate,
        grad_up,
        grad_down,
    )


def solution(mesh):
    return jax.shard_map(
        shards,
        mesh=mesh,
        in_specs=(
            P("dp", None),
            P("dp", None),
            P("dp", None),
            P(),
            P(),
            P(None, "tensor"),
            P(None, "tensor"),
            P(None, "tensor"),
            P("tensor", None),
            P(),
            P(None, "tensor"),
            P(None, "tensor"),
            P("tensor", None),
            P("dp", None),
        ),
        out_specs=(
            P(("dp", "tensor"), None),
            P(("dp", "tensor"), None),
            P(("dp", "tensor")),
            P("dp", "tensor"),
            P("dp", "tensor"),
            P("dp", "tensor"),
            P("tensor", "dp"),
            P(("dp", "tensor")),
            P("dp", "tensor"),
            P("dp", "tensor"),
            P("tensor", "dp"),
        ),
        check_vma=False,
    )
```

```python
import functools

import jax
import jax.numpy as jnp
from jax import lax
from jax.experimental import pallas as pl
from jax.experimental.pallas import tpu as pltpu
from jax.sharding import PartitionSpec as P

HD = 128
CORE, CHIP = 0, 1

epsilon = 1e-05
rope_base = 10000.0


def rope_tables(start):
    length = start.shape[1]
    position = (jnp.arange(length, dtype=jnp.int32) - start[0]).astype(jnp.float32)
    freqs = rope_base ** (-jnp.arange(HD // 2, dtype=jnp.float32) * 2.0 / HD)
    angles = position[:, None] * freqs[None, :]
    cos, sin = jnp.cos(angles), jnp.sin(angles)
    return jnp.concatenate([cos, cos], axis=-1), jnp.concatenate([-sin, sin], axis=-1)


def inv_rms(values):
    return lax.rsqrt(jnp.mean(values * values, axis=-1, keepdims=True) + epsilon)


def product(left, right):
    return jnp.dot(left, right, preferred_element_type=jnp.float32)


def product_tn(left, right):
    return lax.dot_general(
        left, right, (((0,), (0,)), ((), ())), preferred_element_type=jnp.float32
    )


def product_nt(left, right):
    return lax.dot_general(
        left, right, (((1,), (1,)), ((), ())), preferred_element_type=jnp.float32
    )


def norm_back(grad, inputs, inverse, gain):
    weighted = grad * gain
    return inverse * weighted - inputs * inverse**3 * jnp.mean(
        weighted * inputs, axis=-1, keepdims=True
    )


def low(values):
    return values.astype(jnp.bfloat16)


def wide(values):
    return values.astype(jnp.float32)


def part(values, start, stop, dim):
    return lax.slice_in_dim(values, start, stop, axis=dim)


class Chain:
    def __init__(self):
        self.token = None
        self.count = 0
        self.moved = (0, 0)

    def __call__(self, step, *operands):
        if self.token is not None:
            operands, _ = lax.optimization_barrier((operands, self.token))
        self.count += 1
        result = step(*operands)
        self.token = result
        return result

    def move(self, values, axis, pairs):
        values, _ = lax.optimization_barrier((values, self.token))
        if self.moved[0] != self.count:
            self.moved = (self.count, 0)
        part = self.moved[1]
        self.moved = (self.count, part + 1)
        return lax.ppermute(values, axis, pairs)

    def flip(self, values, axis, bit):
        return self.move(values, axis, [(i, i ^ (1 << bit)) for i in range(lax.axis_size(axis))])


class Piece:
    def __init__(self, chain, left, right, width, dim):
        self.chain, self.left, self.right, self.width, self.dim = chain, left, right, width, dim
        self.mine = lax.axis_index("dp")
        self.total = None
        self.todo = list(self.stages)

    def go(self):
        if self.todo:
            stage, self.todo = self.todo[0], self.todo[1:]
            getattr(self, stage)()

    def result(self):
        while self.todo:
            self.go()
        return self.total

    columns_of = None

    def products(self, blocks, dtype, *terms, columns_of=None):
        arrays, places = [t for t, _ in terms], [p for _, p in terms]

        def step(left, right, *arrays):
            return grad(
                left,
                right,
                blocks,
                self.width,
                self.dim,
                dtype,
                list(zip(arrays, places)),
                columns_of,
            )

        return self.chain(step, self.left, self.right, *arrays)


class Halving(Piece):
    def __init__(self, chain, left, right, width, dim, orders, split=()):
        self.orders, self.size = orders, 1 << len(orders[0])
        depth = len(orders[0])
        self.masks = [
            [
                sum(1 << order[s] for s in range(depth) if p >> (depth - 1 - s) & 1)
                for p in range(self.size)
            ]
            for order in orders
        ]
        self.stages, self.sends = [], []
        for step in range(depth):
            half = self.size >> (step + 1)
            cuts = [0, half // 2, half] if step in split and half > 1 else [0, half]
            self.sends += [(step, half, a, b) for a, b in list(zip(cuts, cuts[1:]))[::-1]]
        self.stages = ["send"] * len(self.sends) + ["last"]
        self.received = []
        super().__init__(chain, left, right, width, dim)

    def positions(self, a, b, dtype, **options):
        terms = [(r, a - at) for at, to, r in self.received if at <= a and b <= to]
        core = lax.axis_index("tensor") & 1
        blocks = [
            self.mine ^ (m if m == other else jnp.where(core == 0, m, other))
            for m, other in zip(self.masks[0][a:b], self.masks[1][a:b])
        ]
        return self.products(blocks, dtype, *terms, **options)

    def send(self):
        step, half, a, b = self.sends.pop(0)
        top = self.positions(half + a, half + b, jnp.bfloat16)
        cores = lax.axis_size("tensor")
        pairs = [
            (i * cores + t, (i ^ (1 << self.orders[t & 1][step])) * cores + t)
            for i in range(lax.axis_size("dp"))
            for t in range(cores)
        ]
        self.received.append((a, b, self.chain.move(top, ("dp", "tensor"), pairs)))

    def last(self):
        self.total = self.positions(0, 1, jnp.float32, columns_of=self.columns_of)


def take(values, blocks, width):
    return jnp.concatenate(
        [lax.dynamic_slice_in_dim(values, block * width, width, 1) for block in blocks], axis=1
    )


LOG2E = 1.4426950408889634
SPAN = 512
TILE = 256
COLUMNS = 512
NEG = -1e30


def whole_block(array):
    zeros = (0,) * array.ndim
    return pl.BlockSpec(array.shape, lambda *_: zeros)


def project_kernel(x_ref, gain_ref, wq_ref, wk_ref, wv_ref, cos_ref, sin_ref, n_ref, q_ref, k_ref, v_ref):
    x = wide(x_ref[...])
    inverse = lax.rsqrt(jnp.mean(x * x, axis=-1, keepdims=True) + epsilon)
    normed = low(x * inverse * gain_ref[...])
    n_ref[...] = normed
    cos, sin = cos_ref[...], sin_ref[...]
    for w_ref, o_ref in ((wq_ref, q_ref), (wk_ref, k_ref)):
        linear = product(normed, w_ref[...])
        for h in range(w_ref.shape[1] // HD):
            head = linear[:, h * HD : (h + 1) * HD]
            o_ref[:, h * HD : (h + 1) * HD] = low(head * cos + pltpu.roll(head, HD // 2, 1) * sin)
    v_ref[...] = low(product(normed, wv_ref[...]))


def project(tokens, gain, w_query, w_key, w_value, cos, sin):
    length, model = tokens.shape
    outs = (model, w_query.shape[1], w_key.shape[1], w_value.shape[1])
    rows = lambda columns: pl.BlockSpec((TILE, columns), lambda i: (i, 0))
    gain = gain.reshape(1, model)
    total = sum(outs[1:])
    return pl.pallas_call(
        project_kernel,
        grid=(length // TILE,),
        in_specs=[
            rows(model),
            whole_block(gain),
            whole_block(w_query),
            whole_block(w_key),
            whole_block(w_value),
            rows(HD),
            rows(HD),
        ],
        out_specs=[rows(columns) for columns in outs],
        out_shape=[jax.ShapeDtypeStruct((length, columns), jnp.bfloat16) for columns in outs],
        cost_estimate=pl.CostEstimate(
            flops=2 * length * model * total,
            bytes_accessed=2 * (2 * length * model + model * total + length * total),
            transcendentals=length,
        ),
        name="project",
    )(tokens, gain, w_query, w_key, w_value, cos, sin)


def span(i):
    return max(0, i * TILE - SPAN), (i + 1) * TILE


def allowed_keys(i, start_ref):
    low_key, high_key = span(i)
    shape = (high_key - low_key, TILE)
    key = lax.broadcasted_iota(jnp.int32, shape, 0) + low_key
    query = lax.broadcasted_iota(jnp.int32, shape, 1) + i * TILE
    return (key >= start_ref[:, i * TILE : (i + 1) * TILE]) & (key <= query)


def attend_kernel(half_ref, q_ref, k_ref, v_ref, start_ref, *refs):
    o_ref, lse_ref = refs[-2:]
    scale = HD**-0.5 * LOG2E
    heads = q_ref.shape[1] // HD
    rows = q_ref.shape[0]
    halves = k_ref.shape[0] // rows

    def tile(i):
        low_key, high_key = span(i)
        here = slice(i * TILE % rows, i * TILE % rows + TILE)
        allowed = allowed_keys(i, start_ref)
        values = low(jnp.transpose(wide(v_ref[low_key:high_key, :])))
        for h in range(heads):
            columns = slice(h * HD, (h + 1) * HD)
            logits = product_nt(k_ref[low_key:high_key, :], q_ref[here, columns]) * scale
            logits = jnp.where(allowed, logits, NEG)
            highest = jnp.max(logits, axis=0, keepdims=True)
            weights = jnp.exp2(logits - highest)
            total = jnp.sum(weights, axis=0, keepdims=True)
            probs = low(weights * (1.0 / total))
            o_ref[here, columns] = low(jnp.transpose(product(values, probs)))
            lse_ref[0, h : h + 1, here] = highest + jnp.log2(total)

    for half in range(halves):

        @pl.when(half_ref[0] == half)
        def _():
            for i in range(half * rows // TILE, (half + 1) * rows // TILE):
                tile(i)


def attend(queries, keys, values, start, half, earlier=()):
    length = queries.shape[0]
    rows = length // 2
    kv = keys.shape[1] // HD
    group = queries.shape[1] // keys.shape[1]
    return pl.pallas_call(
        attend_kernel,
        grid_spec=pltpu.PrefetchScalarGridSpec(
            num_scalar_prefetch=1,
            grid=(kv,),
            in_specs=[
                pl.BlockSpec((rows, group * HD), lambda j, half: (half[0], j)),
                pl.BlockSpec((length, HD), lambda j, half: (0, j)),
                pl.BlockSpec((length, HD), lambda j, half: (0, j)),
                whole_block(start),
            ]
            + [pl.BlockSpec(memory_space=pl.ANY)] * len(earlier),
            out_specs=[
                pl.BlockSpec((rows, group * HD), lambda j, half: (half[0], j)),
                pl.BlockSpec((1, group, rows), lambda j, half: (j, 0, half[0])),
            ],
        ),
        out_shape=[
            jax.ShapeDtypeStruct(queries.shape, jnp.bfloat16),
            jax.ShapeDtypeStruct((kv, group, length), jnp.float32),
        ],
        input_output_aliases={5 + i: i for i in range(len(earlier))},
        cost_estimate=pl.CostEstimate(
            flops=2 * length * SPAN * queries.shape[1],
            bytes_accessed=2 * (queries.size + 2 * keys.size),
            transcendentals=length * SPAN * kv * group // 2,
        ),
        name="attend",
    )(half.reshape(1), queries, keys, values, start, *earlier)


def attend_back_kernel(
    kv, q_ref, k_ref, v_ref, start_ref, lse_ref, g_ref, cos_ref, sin_ref, d_ref, k_sum, v_sum
):
    scale = HD**-0.5
    heads = q_ref.shape[1] // HD
    k_sum[...] = jnp.zeros_like(k_sum)
    v_sum[...] = jnp.zeros_like(v_sum)
    k_t = jnp.transpose(wide(k_ref[...]))
    j = pl.program_id(0)

    def columns_at(place):
        return pl.ds(pl.multiple_of(place * HD, HD), HD)

    def unrope(values, here):
        return low(
            values * cos_ref[here, :] - pltpu.roll(values, HD // 2, 1) * sin_ref[here, :]
        )

    for i in range(q_ref.shape[0] // TILE):
        low_key, high_key = span(i)
        here = slice(i * TILE, (i + 1) * TILE)
        reach = slice(low_key, high_key)
        allowed = allowed_keys(i, start_ref)
        for h in range(heads):
            columns = slice(h * HD, (h + 1) * HD)
            query, grad = q_ref[here, columns], g_ref[here, columns]
            logits = product_nt(k_ref[reach, :], query) * (scale * LOG2E)
            logits = jnp.where(allowed, logits - lse_ref[0, h : h + 1, here], NEG)
            probs = jnp.exp2(logits)
            d_probs = product_nt(v_ref[reach, :], grad)
            row_sum = jnp.sum(d_probs * probs, axis=0, keepdims=True)
            d_logits = low(probs * (d_probs - row_sum))
            v_sum[reach, :] += product(low(probs), grad)
            k_sum[reach, :] += product(d_logits, query)
            d_query = jnp.transpose(product(low(k_t[:, reach]), d_logits)) * scale
            d_ref[here, columns_at(j * heads + h)] = unrope(d_query, here)
    everything = slice(0, k_sum.shape[0])
    d_ref[:, columns_at(kv * heads + j)] = unrope(k_sum[...] * scale, everything)
    d_ref[:, columns_at(kv * (heads + 1) + j)] = low(v_sum[...])


def attend_back(queries, keys, values, start, log_total, grads, cos, sin):
    length = queries.shape[0]
    kv = keys.shape[1] // HD
    group = queries.shape[1] // keys.shape[1]
    total = queries.shape[1] + 2 * keys.shape[1]
    wide_block = pl.BlockSpec((length, group * HD), lambda j: (0, j))
    one_block = pl.BlockSpec((length, HD), lambda j: (0, j))
    return pl.pallas_call(
        functools.partial(attend_back_kernel, kv),
        grid=(kv,),
        in_specs=[
            wide_block,
            one_block,
            one_block,
            whole_block(start),
            pl.BlockSpec((1, group, length), lambda j: (j, 0, 0)),
            wide_block,
            whole_block(cos),
            whole_block(sin),
        ],
        out_specs=pl.BlockSpec((length, total), lambda j: (0, 0)),
        out_shape=jax.ShapeDtypeStruct((length, total), jnp.bfloat16),
        scratch_shapes=[pltpu.VMEM((length, HD), jnp.float32)] * 2,
        cost_estimate=pl.CostEstimate(
            flops=5 * length * SPAN * queries.shape[1] * 2,
            bytes_accessed=2 * (3 * queries.size + 4 * keys.size),
            transcendentals=length * SPAN * kv * group,
        ),
        name="attend_back",
    )(queries, keys, values, start, log_total, grads, cos, sin)


def grad_kernel(by_right, outs, blocks_ref, left_ref, right_ref, *refs):
    refs = list(refs)
    turned = refs.pop() if by_right else None
    out_refs, refs = refs[-outs:], refs[:-outs]
    if by_right:

        @pl.when(pl.program_id(0) == 0)
        def _():
            turned[...] = low(jnp.transpose(wide(left_ref[...])))

        total = product(turned[...], right_ref[...])
    else:
        total = product_tn(left_ref[...], right_ref[...])
    for ref in refs:
        total = total + wide(ref[...])
    place = 0
    for out_ref in out_refs:
        columns = out_ref.shape[1]
        out_ref[...] = total[:, place : place + columns].astype(out_ref.dtype)
        place += columns


def grad(left, right, blocks, width, dim, dtype, terms=(), columns_of=None):
    count = len(blocks)
    tokens = left.shape[0]
    rows, columns = left.shape[1], right.shape[1]
    if width % HD:
        if dim == 0:
            left = take(left, blocks, width)
        else:
            right = take(right, blocks, width)
        total = product_tn(left, right)
        for term, place in terms:
            total = total + wide(part(term, place * width, (place + count) * width, dim))
        total = total.astype(dtype)
        if columns_of is None:
            return total
        return jnp.split(total, [sum(columns_of[: i + 1]) for i in range(len(columns_of) - 1)], axis=1)
    by_right = dim == 1
    pick = lambda p, blocks: (0, blocks[p])
    fixed = lambda p, blocks: (0, 0)
    if by_right:
        left_spec, right_spec = pl.BlockSpec((tokens, rows), fixed), pl.BlockSpec((tokens, width), pick)
        shape, block = (rows, count * width), (rows, width)
        at = lambda place: lambda p, blocks: (0, place + p)
    else:
        left_spec, right_spec = pl.BlockSpec((tokens, width), pick), pl.BlockSpec((tokens, columns), fixed)
        shape, block = (count * width, columns), (width, columns)
        at = lambda place: lambda p, blocks: (place + p, 0)
    return pl.pallas_call(
        functools.partial(grad_kernel, by_right, len(columns_of) if columns_of else 1),
        grid_spec=pltpu.PrefetchScalarGridSpec(
            num_scalar_prefetch=1,
            grid=(count,),
            in_specs=[left_spec, right_spec] + [pl.BlockSpec(block, at(place)) for _, place in terms],
            out_specs=[pl.BlockSpec((block[0], c), at(0)) for c in columns_of]
            if columns_of
            else pl.BlockSpec(block, at(0)),
            scratch_shapes=[pltpu.VMEM((rows, tokens), jnp.bfloat16)] if by_right else [],
        ),
        out_shape=[jax.ShapeDtypeStruct((shape[0], c), dtype) for c in columns_of]
        if columns_of
        else jax.ShapeDtypeStruct(shape, dtype),
        cost_estimate=pl.CostEstimate(
            flops=2 * tokens * shape[0] * shape[1],
            bytes_accessed=2 * (tokens * (shape[0] + shape[1]) + (1 + len(terms)) * shape[0] * shape[1]),
            transcendentals=0,
        ),
        name="grad",
    )(jnp.stack(blocks), left, right, *(term for term, _ in terms))


def middle_kernel(place_ref, scale_ref, gain_ref, x_ref, own_ref, near_ref, far_ref, *refs):
    m_ref, inv_ref, n_ref = refs[-3:]
    branch = wide(own_ref[...]) + wide(near_ref[...]) + wide(far_ref[...])
    middle = wide(x_ref[...]) + scale_ref[0] * branch
    inverse = lax.rsqrt(jnp.mean(middle * middle, axis=-1, keepdims=True) + epsilon)
    m_ref[...] = middle
    inv_ref[...] = inverse
    n_ref[...] = low(middle * inverse * gain_ref[...])


def middle_of(chunk, tokens, own, near, far, mine, scale, gain, earlier=()):
    share, model = own.shape
    tile = far.shape[0]
    gain = gain.reshape(1, model)
    at = lambda i, place: (chunk, 0)
    only = lambda i, place: (0, 0)
    return pl.pallas_call(
        middle_kernel,
        grid_spec=pltpu.PrefetchScalarGridSpec(
            num_scalar_prefetch=1,
            grid=(1,),
            in_specs=[
                pl.BlockSpec(memory_space=pltpu.SMEM),
                whole_block(gain),
                pl.BlockSpec((tile, model), lambda i, place: (place[0] * (share // tile) + chunk, 0)),
                pl.BlockSpec((tile, model), at),
                pl.BlockSpec((tile, model), at),
                pl.BlockSpec((tile, model), only),
            ]
            + [pl.BlockSpec(memory_space=pl.ANY)] * len(earlier),
            out_specs=[
                pl.BlockSpec((tile, model), at),
                pl.BlockSpec((tile, 1), at),
                pl.BlockSpec((tile, model), only),
            ],
        ),
        out_shape=[
            jax.ShapeDtypeStruct((share, model), jnp.float32),
            jax.ShapeDtypeStruct((share, 1), jnp.float32),
            jax.ShapeDtypeStruct((tile, model), jnp.bfloat16),
        ],
        input_output_aliases={7 + i: i for i in range(len(earlier))},
        cost_estimate=pl.CostEstimate(
            flops=10 * tile * model, bytes_accessed=14 * tile * model, transcendentals=tile
        ),
        name="middle",
    )(mine.reshape(1), scale.reshape(1), gain, tokens, own, near, far, *earlier)


def gated_kernel(count, places_ref, *refs):
    pieces, (dh_ref, wg_ref, wu_ref) = refs[: 2 * count], refs[2 * count : 2 * count + 3]
    n_ref, hidden_ref, dg_ref, du_ref = refs[-4:]
    core = places_ref[1]

    @pl.when(pl.program_id(0) == 0)
    def _():
        tile = pieces[0].shape[0]
        for i in range(count):
            for place, piece in ((core, pieces[i]), (1 - core, pieces[count + i])):
                row = pl.multiple_of((place * count + i) * tile, tile)
                n_ref[pl.ds(row, tile), :] = piece[...]

    gate = product(n_ref[...], wg_ref[...])
    upward = product(n_ref[...], wu_ref[...])
    d_hidden = dh_ref[...]
    sigma = jax.nn.sigmoid(gate)
    silu = gate * sigma
    hidden_ref[...] = low(silu * upward)
    du_ref[...] = low(d_hidden * silu)
    dg_ref[...] = low(d_hidden * upward * sigma * (1.0 + gate * (1.0 - sigma)))


def gated(chip, core, own, near, d_hidden, w_gate, w_up, earlier=()):
    count = len(own)
    rows = 2 * count * own[0].shape[0]
    length, hidden = d_hidden.shape
    model = w_gate.shape[0]
    whole = lambda array: pl.BlockSpec(array.shape, lambda n, places: (0, 0))
    block = pl.BlockSpec((rows, COLUMNS), lambda n, places: (places[0], n))
    weight = pl.BlockSpec((model, COLUMNS), lambda n, places: (0, n))
    pieces = [*own, *near]
    return pl.pallas_call(
        functools.partial(gated_kernel, count),
        grid_spec=pltpu.PrefetchScalarGridSpec(
            num_scalar_prefetch=1,
            grid=(pl.cdiv(hidden, COLUMNS),),
            in_specs=[whole(piece) for piece in pieces]
            + [block, weight, weight]
            + [pl.BlockSpec(memory_space=pl.ANY)] * len(earlier),
            out_specs=[pl.BlockSpec((rows, model), lambda n, places: (places[0], 0))]
            + [block] * 3,
        ),
        out_shape=[jax.ShapeDtypeStruct((length, model), jnp.bfloat16)]
        + [jax.ShapeDtypeStruct((length, hidden), jnp.bfloat16)] * 3,
        input_output_aliases={4 + 2 * count + i: i for i in range(len(earlier))},
        cost_estimate=pl.CostEstimate(
            flops=4 * rows * model * hidden,
            bytes_accessed=2 * (2 * rows * model + 2 * model * hidden + 5 * rows * hidden),
            transcendentals=rows * hidden,
        ),
        name="gated",
    )(jnp.stack([chip, core]), *pieces, d_hidden, w_gate, w_up, *earlier)


def branch_back_kernel(places_ref, *refs):
    w_ref, d_ref, a_ref = refs[-3:]
    for i, ref in enumerate(refs[:-3]):

        @pl.when(pl.program_id(0) == i)
        def _():
            d_ref[...] = ref[...]

    a_ref[...] = low(product_nt(d_ref[...], w_ref[...]))


def branch_back(pieces, places, w_out):
    rows, model = pieces[0].shape
    count = len(pieces)
    heads = w_out.shape[0]
    fixed = lambda array: pl.BlockSpec(array.shape, lambda p, places: (0, 0))
    return pl.pallas_call(
        branch_back_kernel,
        grid_spec=pltpu.PrefetchScalarGridSpec(
            num_scalar_prefetch=1,
            grid=(count,),
            in_specs=[fixed(piece) for piece in pieces] + [fixed(w_out)],
            out_specs=[
                pl.BlockSpec((rows, model), lambda p, places: (places[p], 0)),
                pl.BlockSpec((rows, heads), lambda p, places: (places[p], 0)),
            ],
        ),
        out_shape=[
            jax.ShapeDtypeStruct((count * rows, model), jnp.bfloat16),
            jax.ShapeDtypeStruct((count * rows, heads), jnp.bfloat16),
        ],
        cost_estimate=pl.CostEstimate(
            flops=2 * count * rows * model * heads,
            bytes_accessed=2 * (2 * count * rows * model + heads * model),
            transcendentals=0,
        ),
        name="branch_back",
    )(jnp.stack(places), *pieces, w_out)


class Scatter:
    def __init__(self, chain, make, left, *operands):
        self.chain, self.make, self.left, self.operands = chain, make, left, operands
        self.share = left[0].shape[0] // 4
        self.mine = lax.axis_index("tensor")
        self.chip, self.core = self.mine >> 1, self.mine & 1

    def rows(self, place, count):
        def step(left, *operands):
            left = [
                lax.dynamic_slice_in_dim(v, place * self.share, count * self.share, 0) for v in left
            ]
            return low(self.make(left, *operands))

        return self.chain(step, self.left, *self.operands)

    def far_half(self):
        self.half = self.rows((1 - self.chip) * 2, 2)
        self.half_near = self.chain.flip(self.half, "tensor", CORE)

    def near_half(self):
        self.own = self.rows(self.chip * 2, 2)
        self.near = self.chain.flip(self.own, "tensor", CORE)

    def far_rows(self):
        self.half_near = self.chain.flip(self.rows(self.mine ^ 3, 1), "tensor", CORE)
        self.half = self.rows(self.mine ^ 2, 1)

    def near_rows(self):
        self.near = self.chain.flip(self.rows(self.mine ^ 1, 1), "tensor", CORE)
        self.own = self.rows(self.mine, 1)

    def mine_of(self, values):
        if values.shape[0] == self.share:
            return values
        return lax.dynamic_slice_in_dim(values, self.core * self.share, self.share, 0)

    def far_send(self):
        total = self.chain(
            lambda a, b: low(wide(self.mine_of(a)) + wide(self.mine_of(b))), self.half, self.half_near
        )
        self.from_far = self.chain.flip(total, "tensor", CHIP)

    def parts(self):
        return self.own, self.near, self.from_far

    def total(self, parts):
        own, near, far = parts
        return wide(self.mine_of(own)) + wide(self.mine_of(near)) + wide(far)


def keep_half(values, axis, dim, bit):
    half = values.shape[dim] // 2
    mine = (lax.axis_index(axis) >> bit) & 1
    return (
        lax.dynamic_slice_in_dim(values, mine * half, half, dim),
        lax.dynamic_slice_in_dim(values, (1 - mine) * half, half, dim),
    )


class SmallScatter:
    def __init__(self, chain, values, dp, ts):
        self.chain, self.values = chain, values
        self.bits = [("tensor", 2, b) for b in range(ts.bit_length() - 1)[::-1]]
        self.bits += [("dp", 1, b) for b in range(dp.bit_length() - 1)[::-1]]
        self.arrived = None

    def step(self):
        if not self.bits:
            return
        (axis, dim, bit), self.bits = self.bits[0], self.bits[1:]

        def halve(values, arrived):
            if arrived is not None:
                values = values + arrived
            return keep_half(values, axis, dim, bit)

        self.values, send = self.chain(halve, self.values, self.arrived)
        self.arrived = self.chain.flip(send, axis, bit)

    def last(self):
        while self.bits:
            self.step()
        return self.chain(lambda a, b: a + b, self.values, self.arrived)[:, 0, 0]


def shards(*arrays):
    return block(Chain(), *arrays)


def block(
    chain,
    tokens,
    segments,
    keep,
    rates,
    gain_attn,
    w_query,
    w_key,
    w_value,
    w_out,
    gain_ffn,
    w_gate,
    w_up,
    w_down,
    cotangent,
):
    length, model = tokens.shape
    dp = lax.axis_size("dp")
    ts = lax.axis_size("tensor")
    share = length // ts
    mine = lax.axis_index("tensor")
    chip, core = mine >> 1, mine & 1
    first = mine * share
    width = model // dp
    segs = segments[0]
    start = jnp.sum((segs[:, None] < segs[None, :]).astype(jnp.int32), axis=0, keepdims=True)
    cos, sin = rope_tables(start)

    normed, queries, keys, values = chain(
        project, tokens, gain_attn, w_query, w_key, w_value, cos, sin
    )
    earlier = chain(attend, queries, keys, values, start, 1 - chip)
    branch = Scatter(chain, lambda left, w: product(left[0], w), [earlier[0]], w_out)
    branch.far_rows()
    tile = share // 2
    chunks = [(c * tile, (c + 1) * tile, 0) for c in range(2)]
    totals = chain(
        lambda a, b: [low(wide(part(a, *c)) + wide(part(b, *c))) for c in chunks],
        branch.half,
        branch.half_near,
    )
    arrived = [chain.flip(total, "tensor", CHIP) for total in totals]
    attended, log_total = chain(
        lambda *o: attend(*o[:5], o[5]), queries, keys, values, start, chip, tuple(earlier)
    )
    branch.left = [attended]
    branch.near_rows()

    def prepare(keep, rates, cotangent):
        scales = keep[0].astype(jnp.float32) / rates
        return scales[0], scales[1], low(scales[1] * wide(cotangent))

    scale_attn, scale_ffn, d_ffn = chain(prepare, keep, rates, cotangent)
    far, near, own, outs = [], [], [], ()
    for c in range(2):
        *outs, normed_rows = chain(
            lambda *o: middle_of(c, *o),
            tokens,
            branch.own,
            branch.near,
            arrived[c],
            mine,
            scale_attn,
            gain_ffn,
            tuple(outs),
        )
        own.append(normed_rows)
        far.append(chain.flip(normed_rows, "tensor", CHIP))
        near.append(chain.flip(normed_rows, "tensor", CORE))
        if c == 0:
            d_hidden = chain(product_nt, d_ffn, w_down)
    middle_rows, inv_mid_rows = outs
    outs = chain(gated, chip, core, own, near, d_hidden, w_gate, w_up)
    far_near = [chain.flip(f, "tensor", CORE) for f in far]
    normed_ffn, hidden, d_gate, d_up = chain(
        gated, 1 - chip, core, far, far_near, d_hidden, w_gate, w_up, tuple(outs)
    )
    bits = list(range(dp.bit_length() - 1))
    swapped = bits[:1] + bits[1:3][::-1] + bits[3:]

    def over_dp(left, right, dim, split=(), order=lambda v: v):
        return Halving(chain, left, right, width, dim, (order(bits), order(swapped)), split)

    gate_g = over_dp(normed_ffn, d_gate, 0)
    up_g = over_dp(normed_ffn, d_up, 0)
    down_g = over_dp(hidden, d_ffn, 1, split=(1,), order=lambda v: [v[1], v[0]] + v[2:])
    gate_g.go()
    down_g.go()

    d_normed = Scatter(
        chain,
        lambda left, g, u: product_nt(left[0], g) + product_nt(left[1], u),
        [d_gate, d_up],
        w_gate,
        w_up,
    )
    ffn = Scatter(chain, lambda left, w: product(left[0], w), [hidden], w_down)
    d_normed.far_half()
    up_g.go()
    d_normed.far_send()
    d_normed.near_half()
    ffn.far_half()

    def middle_back(parts, middle_rows, inv_mid_rows, cotangent):
        d_normed_rows = d_normed.total(parts)
        grad_rows = wide(lax.dynamic_slice_in_dim(cotangent, first, share, 0))
        d_middle_rows = grad_rows + norm_back(d_normed_rows, middle_rows, inv_mid_rows, gain_ffn)
        gain_ffn_part = jnp.sum(d_normed_rows * middle_rows * inv_mid_rows, axis=0)
        return d_middle_rows, low(scale_attn * d_middle_rows), gain_ffn_part

    d_middle_rows, d_branch_rows, gain_ffn_part = chain(
        middle_back, d_normed.parts(), middle_rows, inv_mid_rows, cotangent
    )
    far = chain.flip(d_branch_rows, "tensor", CHIP)
    near = chain.flip(d_branch_rows, "tensor", CORE)
    ffn.far_send()
    gate_g.go()
    ffn.near_half()
    far_near = chain.flip(far, "tensor", CORE)
    d_branch, d_attended = chain(
        lambda *o: branch_back(o[:4], [mine, mine ^ 1, mine ^ 2, mine ^ 3], o[4]),
        d_branch_rows,
        near,
        far,
        far_near,
        w_out,
    )
    wout_g = over_dp(attended, d_branch, 1)
    wout_g.go()
    gate_g.go()
    d_qkv = chain(attend_back, queries, keys, values, start, log_total, d_attended, cos, sin)
    qkv_g = over_dp(normed, d_qkv, 0, split=(0, 1))
    qkv_g.columns_of = (w_query.shape[1], w_key.shape[1], w_value.shape[1])
    up_g.go()
    qkv_g.go()
    down_g.go()
    qkv_g.go()
    down_g.go()
    q_cols, k_cols = w_query.shape[1], w_key.shape[1]

    def d_first_of(left, w_query, w_key, w_value):
        d_rows = left[0]
        return (
            product_nt(d_rows[:, :q_cols], w_query)
            + product_nt(d_rows[:, q_cols : q_cols + k_cols], w_key)
            + product_nt(d_rows[:, q_cols + k_cols :], w_value)
        )

    d_first = Scatter(chain, d_first_of, [d_qkv], w_query, w_key, w_value)
    d_first.far_rows()
    wout_g.go()
    d_first.far_send()
    d_first.near_rows()
    qkv_g.go()
    qkv_g.go()
    up_g.go()
    down_g.go()
    wout_g.go()

    def input_back(parts, tokens, d_middle_rows):
        d_first_rows = d_first.total(parts)
        input_rows = wide(lax.dynamic_slice_in_dim(tokens, first, share, 0))
        inv_in_rows = inv_rms(input_rows)
        tokens_grad = d_middle_rows + norm_back(d_first_rows, input_rows, inv_in_rows, gain_attn)
        return tokens_grad, jnp.sum(d_first_rows * input_rows * inv_in_rows, axis=0)

    tokens_grad, gain_attn_part = chain(input_back, d_first.parts(), tokens, d_middle_rows)
    gains = SmallScatter(
        chain, jnp.stack([gain_attn_part, gain_ffn_part]).reshape(2, dp, ts, -1), dp, ts
    )
    gains.step()
    gains.step()
    gains.step()
    qkv_g.go()
    layer_out = chain(lambda m, f: m + scale_ffn * ffn.total(f), middle_rows, ffn.parts())
    grad_gate = gate_g.result() if len(bits) == 3 else None
    grad_down = down_g.result()
    gains.step()
    for _ in range(len(bits) - 3):
        for piece in (gate_g, up_g, wout_g, qkv_g):
            piece.go()
    if grad_gate is None:
        grad_gate = gate_g.result()
    grad_up = up_g.result()
    grad_wout = wout_g.result()
    gains.step()
    grad_query, grad_key, grad_value = qkv_g.result()
    gains = gains.last()
    return (
        layer_out,
        tokens_grad,
        gains[0],
        grad_query,
        grad_key,
        grad_value,
        grad_wout,
        gains[1],
        grad_gate,
        grad_up,
        grad_down,
    )


def solution(mesh):
    return jax.shard_map(
        shards,
        mesh=mesh,
        in_specs=(
            P("dp", None),
            P("dp", None),
            P("dp", None),
            P(),
            P(),
            P(None, "tensor"),
            P(None, "tensor"),
            P(None, "tensor"),
            P("tensor", None),
            P(),
            P(None, "tensor"),
            P(None, "tensor"),
            P("tensor", None),
            P("dp", None),
        ),
        out_specs=(
            P(("dp", "tensor"), None),
            P(("dp", "tensor"), None),
            P(("dp", "tensor")),
            P("dp", "tensor"),
            P("dp", "tensor"),
            P("dp", "tensor"),
            P("tensor", "dp"),
            P(("dp", "tensor")),
            P("dp", "tensor"),
            P("dp", "tensor"),
            P("tensor", "dp"),
        ),
        check_vma=False,
    )
```
